1024 devices in a mesh: row: 64 (over x, y), col: 16 (over z, core).
Axes of the slice: x: 8, y: 8, z: 8, core: 2. Of those that a mesh axis runs over, the one named last changes fastest.
Arguments:
- similarity: bfloat16 [7168, 7168], P('row', 'col'), may hold values from 0.0099487305 to 1
- in_pattern: int32 [56, 56], replicated, may hold values 0 or 1
- out_pattern: int32 [56, 56], replicated, may hold values 0 or 1
Outputs:
- inflated: bfloat16 [7168, 7168], P('row', 'col')
The draws below stay inside these ranges and needn't reach their ends.
All inputs are finite; a program needn't handle non-finite values.
Results may differ from the reference program's by a relative error of at most 0.0029.
Values may be sent and summed in bfloat16 or wider, within the bound.
No kernel may reach another device: no remote copies, remote signals or barrier semaphores. Data moves between devices by JAX's collectives and lax.ppermute only.
A program may use at most 32 MiB of HBM per device.

```python
import math
import jax
import jax.numpy as jnp

BLK = 128
N = 7168
NB = 56


def touch_ends(array, stream_key, smallest, largest):
    spot = [jax.random.randint(jax.random.fold_in(stream_key, axis), (), 0, length) for axis, length in enumerate(array.shape)]
    main_axis = array.shape.index(max(array.shape))
    beside = spot[:main_axis] + [(spot[main_axis] + 1) % array.shape[main_axis]] + spot[main_axis + 1:]
    return array.at[tuple(spot)].set(smallest).at[tuple(beside)].set(largest)


def levels(rng, dims, cuts, low, top_value):
    factor_of = 1.0
    for position, parts in cuts:
        heights = jax.random.uniform(jax.random.fold_in(jax.random.fold_in(rng, 6), position), (parts,), jnp.float32, low / len(cuts), top_value / len(cuts))
        factor_of = factor_of * jnp.repeat(jnp.exp(heights), dims[position] // parts).reshape((-1,) + (1,) * (len(dims) - 1 - position))
    return factor_of


def setup_inputs(seed: int = 0) -> dict:
    streams_of = jax.random.split(jax.random.key(seed), 4)
    return {
        "similarity": jnp.clip(jnp.exp(math.log(1.0) - 4.61031033 * jax.random.uniform(streams_of[0], (N, N), jnp.float32) ** levels(streams_of[0], (N, N), ((0, 64), (1, 16)), -0.2, 0.2)), 0.0099487305, 1.0).astype(jnp.bfloat16),
        "in_pattern": touch_ends((jax.random.randint(streams_of[1], (NB, NB), 0, 4) < 3).astype(jnp.int32), jax.random.fold_in(streams_of[1], 1), 0, 1),
        "out_pattern": touch_ends((jax.random.randint(streams_of[2], (NB, NB), 0, 2) < 1).astype(jnp.int32), jax.random.fold_in(streams_of[2], 1), 0, 1),
    }


def expand_mask(pattern):
    forced = jnp.maximum(pattern, jnp.eye(NB, dtype=jnp.int32))
    return jnp.repeat(jnp.repeat(forced, BLK, axis=0), BLK, axis=1) > 0


def reference(similarity, in_pattern, out_pattern):
    masked = jnp.where(expand_mask(in_pattern), similarity.astype(jnp.float32), jnp.float32(0.0))
    in_sums = jnp.sum(masked, axis=0)
    stochastic = (masked / in_sums[None, :]).astype(jnp.bfloat16)
    product = jnp.dot(stochastic, stochastic, preferred_element_type=jnp.float32)
    expanded = jnp.where(expand_mask(out_pattern), product, jnp.float32(0.0))
    squared = expanded * expanded
    out_sums = jnp.sum(squared, axis=0)
    return (jnp.float32(N) * squared / out_sums[None, :]).astype(jnp.bfloat16)
```

```python
import jax
import jax.numpy as jnp
from jax import lax
from jax.sharding import Mesh
from jax.sharding import PartitionSpec as P

BLK = 128
F32 = jnp.float32
BF16 = jnp.bfloat16
SCALE = 64.0


def local_mask(pattern, row_start, rows, col_start, cols):
    blocks = pattern.shape[0]
    row_blocks = (row_start + lax.broadcasted_iota(jnp.int32, (rows, blocks), 0)) // BLK
    pick_row = (row_blocks == lax.broadcasted_iota(jnp.int32, (rows, blocks), 1)).astype(BF16)
    col_blocks = (col_start + lax.broadcasted_iota(jnp.int32, (blocks, cols), 1)) // BLK
    pick_col = (col_blocks == lax.broadcasted_iota(jnp.int32, (blocks, cols), 0)).astype(BF16)
    eye = jnp.eye(blocks, dtype=jnp.int32)
    kept = jnp.maximum(pattern, eye).astype(BF16)
    by_row = jnp.dot(pick_row, kept, preferred_element_type=F32).astype(BF16)
    return jnp.dot(by_row, pick_col, preferred_element_type=F32) > 0.5


def split3(v):
    hi = v.astype(BF16)
    rest = v - hi.astype(F32)
    mid = rest.astype(BF16)
    low = (rest - mid.astype(F32)).astype(BF16)
    z = jnp.zeros_like(hi)
    return jnp.stack([hi, mid, low, z, z, z, z, z])


def body(similarity, in_pattern, out_pattern):
    rows, cols = similarity.shape
    x, y = lax.axis_index("x"), lax.axis_index("y")
    z, core = lax.axis_index("z"), lax.axis_index("core")
    n = lax.axis_size("x")
    order = rows * n * n
    row_start = (x * n + y) * rows
    col_start = (z * 2 + core) * cols
    in_mask = local_mask(in_pattern, row_start, rows, col_start, cols)
    masked = jnp.where(in_mask, similarity, jnp.zeros_like(similarity))
    swap = [(i * n + j, j * n + i) for i in range(n) for j in range(n)]
    left = lax.ppermute(masked, ("y", "z"), swap)
    right = lax.ppermute(masked, ("x", "y"), swap)
    own_sums = jnp.sum(masked.astype(F32), axis=0)
    part = jnp.sum(left.astype(F32), axis=0)
    right_all = lax.all_gather(jnp.concatenate([right, split3(part)]), "x")
    part = jnp.sum(right_all[:, rows : rows + 3].astype(F32), axis=(0, 1))
    left_all = lax.all_gather(jnp.concatenate([left, split3(part)]), "z")
    in_sums = jnp.sum(left_all[:, rows : rows + 3].astype(F32), axis=(0, 1))
    left_own = (left_all[:, :rows].astype(F32) / in_sums).astype(BF16).reshape(n * rows, cols)
    left_other = lax.ppermute(left_own, "core", [(0, 1), (1, 0)])
    halves = right_all[:, :rows].reshape(2, cols, cols)
    right_own = lax.dynamic_index_in_dim(halves, core, 0, False)
    right_other = lax.dynamic_index_in_dim(halves, 1 - core, 0, False)
    partial = jnp.dot(left_own, right_own, preferred_element_type=F32)
    partial = partial + jnp.dot(left_other, right_other, preferred_element_type=F32)
    partial = (partial * F32(SCALE)).astype(jnp.float16).reshape(n, rows, cols)
    partials = lax.all_to_all(partial, "y", 0, 0)
    product = jnp.sum(partials.astype(F32), axis=0) * F32(1.0 / SCALE)
    out_mask = local_mask(out_pattern, row_start, rows, col_start, cols)
    product = jnp.where(out_mask, product, F32(0.0))
    sums = jnp.concatenate([jnp.sum(product * product, axis=0), own_sums, jnp.zeros((1024 - 2 * cols,), F32)])
    sums = jnp.broadcast_to(sums.reshape(1, 8, 128), (n * n, 8, 128))
    sums = jnp.sum(lax.all_to_all(sums, ("x", "y"), 0, 0), axis=0).reshape(1024)
    own_in = sums[cols : 2 * cols]
    expanded = product / own_in
    out_sums = sums[:cols] / (own_in * own_in)
    return (F32(order) * (expanded * expanded) / out_sums).astype(BF16)


def solution(mesh):
    fine = Mesh(mesh.devices.reshape(8, 8, 8, 2), ("x", "y", "z", "core"))
    cells = P(("x", "y"), ("z", "core"))
    return jax.shard_map(
        body, mesh=fine, in_specs=(cells, P(), P()), out_specs=cells, check_vma=False
    )
```

```python
import jax
import jax.numpy as jnp
from jax import lax
from jax.sharding import Mesh
from jax.sharding import PartitionSpec as P

BLK = 128
F32 = jnp.float32
BF16 = jnp.bfloat16
SCALE = 64.0


def local_mask(pattern, row_start, rows, col_start, cols):
    blocks = pattern.shape[0]
    row_blocks = (row_start + lax.broadcasted_iota(jnp.int32, (rows, blocks), 0)) // BLK
    pick_row = (row_blocks == lax.broadcasted_iota(jnp.int32, (rows, blocks), 1)).astype(BF16)
    col_blocks = (col_start + lax.broadcasted_iota(jnp.int32, (blocks, cols), 1)) // BLK
    pick_col = (col_blocks == lax.broadcasted_iota(jnp.int32, (blocks, cols), 0)).astype(BF16)
    eye = jnp.eye(blocks, dtype=jnp.int32)
    kept = jnp.maximum(pattern, eye).astype(BF16)
    by_row = jnp.dot(pick_row, kept, preferred_element_type=F32).astype(BF16)
    return jnp.dot(by_row, pick_col, preferred_element_type=F32) > 0.5


def body(similarity, in_pattern, out_pattern):
    rows, cols = similarity.shape
    x, y = lax.axis_index("x"), lax.axis_index("y")
    z, core = lax.axis_index("z"), lax.axis_index("core")
    n = lax.axis_size("x")
    order = rows * n * n
    row_start = (x * n + y) * rows
    col_start = (z * 2 + core) * cols
    in_mask = local_mask(in_pattern, row_start, rows, col_start, cols)
    masked = jnp.where(in_mask, similarity, jnp.zeros_like(similarity))
    half = rows // 2
    low, high = masked[:half], masked[half:]
    front = y < n // 2
    first = lax.ppermute(
        jnp.where(front, low, high), "y", [(i, 2 * i) if i < n // 2 else (i, 2 * i - n + 1) for i in range(n)]
    )
    second = lax.ppermute(
        jnp.where(front, high, low), "y", [(i, 2 * i + 1) if i < n // 2 else (i, 2 * i - n) for i in range(n)]
    )
    own_sums = jnp.sum(masked.astype(F32), axis=0)
    left = jnp.broadcast_to(masked.T.reshape(n, 1, half, rows), (n, n, half, rows))
    left = lax.all_to_all(left.reshape(n * n, half, rows), ("y", "z"), 0, 0)
    left = left.reshape(n, cols, rows)
    part = jnp.sum(left.astype(F32), axis=(0, 2))
    part = jnp.concatenate([part, jnp.zeros((512 - cols,), F32)]).reshape(1, 4, 128)
    in_sums = lax.all_to_all(jnp.broadcast_to(part, (n, 4, 128)), "x", 0, 0)
    in_sums = jnp.sum(in_sums, axis=0).reshape(512)[:cols]
    right_all = lax.all_gather(jnp.concatenate([first, second]), "x")
    left_own = (left.astype(F32) / in_sums[None, :, None]).astype(BF16)
    left_other = lax.ppermute(left_own, "core", [(0, 1), (1, 0)])
    slot = (core + y) % 2
    halves = right_all.reshape(n, 2, half, cols)
    right_own = lax.dynamic_index_in_dim(halves, slot, 1, False).reshape(cols, cols)
    right_other = lax.dynamic_index_in_dim(halves, 1 - slot, 1, False).reshape(cols, cols)
    over_k = (((1,), (0,)), ((), ()))
    partial = lax.dot_general(left_own, right_own, over_k, preferred_element_type=F32)
    partial = partial + lax.dot_general(left_other, right_other, over_k, preferred_element_type=F32)
    partial = (partial * F32(SCALE)).astype(jnp.float16).reshape(n, rows, cols)
    partials = lax.all_to_all(partial, "y", 0, 0)
    product = jnp.sum(partials.astype(F32), axis=0) * F32(1.0 / SCALE)
    out_mask = local_mask(out_pattern, row_start, rows, col_start, cols)
    product = jnp.where(out_mask, product, F32(0.0))
    sums = jnp.concatenate([jnp.sum(product * product, axis=0), own_sums, jnp.zeros((1024 - 2 * cols,), F32)])
    sums = sums.reshape(8, 128)
    for axis in ("y", "x"):
        sums = jnp.sum(lax.all_to_all(jnp.broadcast_to(sums, (n, 8, 128)), axis, 0, 0), axis=0)
    sums = sums.reshape(1024)
    own_in = sums[cols : 2 * cols]
    expanded = product / own_in
    out_sums = sums[:cols] / (own_in * own_in)
    return (F32(order) * (expanded * expanded) / out_sums).astype(BF16)


def solution(mesh):
    fine = Mesh(mesh.devices.reshape(8, 8, 8, 2), ("x", "y", "z", "core"))
    cells = P(("x", "y"), ("z", "core"))
    return jax.shard_map(
        body, mesh=fine, in_specs=(cells, P(), P()), out_specs=cells, check_vma=False
    )
```

```python
import jax
import jax.numpy as jnp
from jax import lax
from jax.sharding import Mesh
from jax.sharding import PartitionSpec as P

BLK = 128
F32 = jnp.float32
BF16 = jnp.bfloat16
SCALE = 64.0


def local_mask(pattern, row_start, rows, col_start, cols):
    blocks = pattern.shape[0]
    row_blocks = (row_start + lax.broadcasted_iota(jnp.int32, (rows, blocks), 0)) // BLK
    pick_row = (row_blocks == lax.broadcasted_iota(jnp.int32, (rows, blocks), 1)).astype(BF16)
    col_blocks = (col_start + lax.broadcasted_iota(jnp.int32, (blocks, cols), 1)) // BLK
    pick_col = (col_blocks == lax.broadcasted_iota(jnp.int32, (blocks, cols), 0)).astype(BF16)
    eye = jnp.eye(blocks, dtype=jnp.int32)
    kept = jnp.maximum(pattern, eye).astype(BF16)
    by_row = jnp.dot(pick_row, kept, preferred_element_type=F32).astype(BF16)
    return jnp.dot(by_row, pick_col, preferred_element_type=F32) > 0.5


def send_all(v, axes, count):
    return jnp.sum(lax.all_to_all(jnp.broadcast_to(v, (count,) + v.shape), axes, 0, 0), axis=0)


def body(similarity, in_pattern, out_pattern):
    rows, cols = similarity.shape
    x, quad, spot = lax.axis_index("x"), lax.axis_index("quad"), lax.axis_index("spot")
    z, core = lax.axis_index("z"), lax.axis_index("core")
    n, m = lax.axis_size("x"), lax.axis_size("spot")
    order = rows * n * n
    row_start = (x * n + quad * m + spot) * rows
    col_start = (z * 2 + core) * cols
    in_mask = local_mask(in_pattern, row_start, rows, col_start, cols)
    masked = jnp.where(in_mask, similarity, jnp.zeros_like(similarity))
    own_sums = jnp.sum(masked.astype(F32), axis=0)

    left = lax.ppermute(masked, ("quad", "core"), [(0, 0), (1, 2), (2, 1), (3, 3)])
    left = jnp.broadcast_to(left.T.reshape(m, 1, rows, rows), (m, n, rows, rows))
    left = lax.all_to_all(left.reshape(m * n, rows, rows), ("spot", "z"), 0, 0)
    left = left.reshape(m, n, rows, rows)
    right = lax.all_gather(masked, "x", tiled=True)

    left, right = lax.optimization_barrier((left, right))
    other = lax.ppermute(left, "core", [(0, 1), (1, 0)])
    part = jnp.sum(left.astype(F32), axis=(0, 3))
    part = jnp.pad(part, ((0, 0), (0, 128 - rows)))
    in_sums = send_all(part, ("x", "core"), 2 * n)[:, :rows, None]

    def times(l):
        l = (l.astype(F32) / in_sums).astype(BF16).reshape(m, n * rows, rows)
        p = lax.dot_general(l, right, (((1,), (0,)), ((), ())), preferred_element_type=F32)
        return (p * F32(SCALE)).astype(jnp.float16)

    own, other = times(left), times(other)
    partial = jnp.where(core == 0, jnp.concatenate([own, other]), jnp.concatenate([other, own]))
    partials = lax.all_to_all(partial, ("quad", "spot"), 0, 0)
    product = jnp.sum(partials.astype(F32), axis=0) * F32(1.0 / SCALE)
    out_mask = local_mask(out_pattern, row_start, rows, col_start, cols)
    product = jnp.where(out_mask, product, F32(0.0))
    sums = jnp.concatenate([jnp.sum(product * product, axis=0), own_sums, jnp.zeros((1024 - 2 * cols,), F32)])
    sums = send_all(send_all(sums.reshape(8, 128), ("quad", "spot"), n), "x", n).reshape(1024)
    own_in = sums[cols : 2 * cols]
    expanded = product / own_in
    out_sums = sums[:cols] / (own_in * own_in)
    return (F32(order) * (expanded * expanded) / out_sums).astype(BF16)


def solution(mesh):
    fine = Mesh(mesh.devices.reshape(8, 2, 4, 8, 2), ("x", "quad", "spot", "z", "core"))
    cells = P(("x", "quad", "spot"), ("z", "core"))
    return jax.shard_map(
        body, mesh=fine, in_specs=(cells, P(), P()), out_specs=cells, check_vma=False
    )
```

```python
import jax
import jax.numpy as jnp
from jax import lax
from jax.sharding import Mesh
from jax.sharding import PartitionSpec as P

BLK = 128
F32 = jnp.float32
BF16 = jnp.bfloat16
SCALE = 64.0


def local_mask(pattern, row_start, rows, col_start, cols):
    blocks = pattern.shape[0]
    row_blocks = (row_start + lax.broadcasted_iota(jnp.int32, (rows, blocks), 0)) // BLK
    pick_row = (row_blocks == lax.broadcasted_iota(jnp.int32, (rows, blocks), 1)).astype(BF16)
    col_blocks = (col_start + lax.broadcasted_iota(jnp.int32, (blocks, cols), 1)) // BLK
    pick_col = (col_blocks == lax.broadcasted_iota(jnp.int32, (blocks, cols), 0)).astype(BF16)
    eye = jnp.eye(blocks, dtype=jnp.int32)
    kept = jnp.maximum(pattern, eye).astype(BF16)
    by_row = jnp.dot(pick_row, kept, preferred_element_type=F32).astype(BF16)
    return jnp.dot(by_row, pick_col, preferred_element_type=F32) > 0.5


def send_all(v, axes, count):
    return jnp.sum(lax.all_to_all(jnp.broadcast_to(v, (count,) + v.shape), axes, 0, 0), axis=0)


def multiply(similarity, in_pattern):
    rows, cols = similarity.shape
    x, quad, spot = lax.axis_index("x"), lax.axis_index("quad"), lax.axis_index("spot")
    z, core = lax.axis_index("z"), lax.axis_index("core")
    n, m = lax.axis_size("x"), lax.axis_size("spot")
    row_start = (x * n + quad * m + spot) * rows
    col_start = (z * 2 + core) * cols
    in_mask = local_mask(in_pattern, row_start, rows, col_start, cols)
    masked = jnp.where(in_mask, similarity, jnp.zeros_like(similarity))
    own_sums = jnp.sum(masked.astype(F32), axis=0)

    left = lax.ppermute(masked, ("quad", "core"), [(0, 0), (1, 2), (2, 1), (3, 3)])
    left = jnp.broadcast_to(left.T.reshape(m, 1, rows, rows), (m, n, rows, rows))
    left = lax.all_to_all(left.reshape(m * n, rows, rows), ("spot", "z"), 0, 0)
    left = left.reshape(m, n, rows, rows)
    right = lax.all_gather(masked, "x", tiled=True)

    left, right = lax.optimization_barrier((left, right))
    other = lax.ppermute(left, "core", [(0, 1), (1, 0)])
    part = jnp.sum(left.astype(F32), axis=(0, 3)) + jnp.sum(other.astype(F32), axis=(0, 3))
    part = jnp.pad(part, ((0, 0), (0, 128 - rows)))
    in_sums = send_all(part, "x", n)[:, :rows, None]
    left = jnp.where(core == 0, jnp.concatenate([left, other]), jnp.concatenate([other, left]))
    left = (left.astype(F32) / in_sums).astype(BF16).reshape(n, n * rows, rows)
    partial = lax.dot_general(left, right, (((1,), (0,)), ((), ())), preferred_element_type=F32)
    partial = (partial * F32(SCALE)).astype(jnp.float16)
    return partial.reshape(n * rows, cols), own_sums.reshape(1, cols)


def finish(partial, own_sums, out_pattern):
    x, y = lax.axis_index("x"), lax.axis_index("y")
    z, core = lax.axis_index("z"), lax.axis_index("core")
    n = lax.axis_size("x")
    rows, cols = partial.shape[0] // n, partial.shape[1]
    order = rows * n * n
    partials = lax.all_to_all(partial.reshape(n, rows, cols), "y", 0, 0)
    product = jnp.sum(partials.astype(F32), axis=0) * F32(1.0 / SCALE)
    out_mask = local_mask(out_pattern, (x * n + y) * rows, rows, (z * 2 + core) * cols, cols)
    product = jnp.where(out_mask, product, F32(0.0))
    sums = jnp.concatenate(
        [jnp.sum(product * product, axis=0), own_sums.reshape(cols), jnp.zeros((1024 - 2 * cols,), F32)]
    )
    sums = send_all(send_all(sums.reshape(8, 128), "y", n), "x", n).reshape(1024)
    own_in = sums[cols : 2 * cols]
    expanded = product / own_in
    out_sums = sums[:cols] / (own_in * own_in)
    return (F32(order) * (expanded * expanded) / out_sums).astype(BF16)


def solution(mesh):
    cut = Mesh(mesh.devices.reshape(8, 2, 4, 8, 2), ("x", "quad", "spot", "z", "core"))
    whole = Mesh(mesh.devices.reshape(8, 8, 8, 2), ("x", "y", "z", "core"))
    cells_cut = P(("x", "quad", "spot"), ("z", "core"))
    cells = P(("x", "y"), ("z", "core"))
    first = jax.shard_map(
        multiply, mesh=cut, in_specs=(cells_cut, P()), out_specs=(cells_cut, cells_cut), check_vma=False
    )
    second = jax.shard_map(
        finish, mesh=whole, in_specs=(cells, cells, P()), out_specs=cells, check_vma=False
    )

    def step(similarity, in_pattern, out_pattern):
        return second(*first(similarity, in_pattern), out_pattern)

    return step
```

```python
import jax
import jax.numpy as jnp
from jax import lax
from jax.sharding import Mesh
from jax.sharding import PartitionSpec as P


BLK = 128
F32 = jnp.float32
BF16 = jnp.bfloat16
SCALE = 64.0


def local_mask(pattern, row_start, rows, col_start, cols):
    blocks = pattern.shape[0]
    row_blocks = (row_start + lax.broadcasted_iota(jnp.int32, (rows, blocks), 0)) // BLK
    pick_row = (row_blocks == lax.broadcasted_iota(jnp.int32, (rows, blocks), 1)).astype(BF16)
    col_blocks = (col_start + lax.broadcasted_iota(jnp.int32, (blocks, cols), 1)) // BLK
    pick_col = (col_blocks == lax.broadcasted_iota(jnp.int32, (blocks, cols), 0)).astype(BF16)
    eye = jnp.eye(blocks, dtype=jnp.int32)
    kept = jnp.maximum(pattern, eye).astype(BF16)
    by_row = jnp.dot(pick_row, kept, preferred_element_type=F32).astype(BF16)
    return jnp.dot(by_row, pick_col, preferred_element_type=F32) > 0.5


def body(similarity, in_pattern, out_pattern):
    rows, cols = similarity.shape
    x, y = lax.axis_index("x"), lax.axis_index("y")
    z, core = lax.axis_index("z"), lax.axis_index("core")
    n = lax.axis_size("x")
    order = rows * n * n
    row_start = (x * n + y) * rows
    col_start = (z * 2 + core) * cols
    in_mask = local_mask(in_pattern, row_start, rows, col_start, cols)
    masked = jnp.where(in_mask, similarity, jnp.zeros_like(similarity))
    half = rows // 2
    front = y < n // 2
    low, high = masked[:half], masked[half:]
    first = lax.ppermute(
        jnp.where(front, low, high), "y", [(i, 2 * i) if i < n // 2 else (i, 2 * i - n + 1) for i in range(n)]
    )
    second = lax.ppermute(
        jnp.where(front, high, low), "y", [(i, 2 * i + 1) if i < n // 2 else (i, 2 * i - n) for i in range(n)]
    )
    own_sums = jnp.sum(masked.astype(F32), axis=0)
    left = jnp.broadcast_to(masked.T.reshape(n, 1, half, rows), (n, n, half, rows))
    left = lax.all_to_all(left.reshape(n * n, half, rows), ("y", "z"), 0, 0)
    left = left.reshape(n, cols, rows)
    right_all = lax.all_gather(jnp.concatenate([first, second]), "x")
    left, right_all = lax.optimization_barrier((left, right_all))
    part = jnp.sum(left.astype(F32), axis=(0, 2))
    part = jnp.concatenate([part, jnp.zeros((512 - cols,), F32)]).reshape(1, 4, 128)
    in_sums = lax.all_to_all(jnp.broadcast_to(part, (n, 4, 128)), "x", 0, 0)
    in_sums = jnp.sum(in_sums, axis=0).reshape(512)[:cols]
    left_own = (left.astype(F32) / in_sums[None, :, None]).astype(BF16)
    left_other = lax.ppermute(left_own, "core", [(0, 1), (1, 0)])
    slot = (core + y) % 2
    halves = right_all.reshape(n, 2, half, cols)
    right_own = lax.dynamic_index_in_dim(halves, slot, 1, False).reshape(cols, cols)
    right_other = lax.dynamic_index_in_dim(halves, 1 - slot, 1, False).reshape(cols, cols)
    over_k = (((1,), (0,)), ((), ()))
    partial = lax.dot_general(left_own, right_own, over_k, preferred_element_type=F32)
    partial = partial + lax.dot_general(left_other, right_other, over_k, preferred_element_type=F32)
    partial = (partial * F32(SCALE)).astype(jnp.float16).reshape(n, rows, cols)
    partials = lax.all_to_all(partial, "y", 0, 0)
    product = jnp.sum(partials.astype(F32), axis=0) * F32(1.0 / SCALE)
    out_mask = local_mask(out_pattern, row_start, rows, col_start, cols)
    product = jnp.where(out_mask, product, F32(0.0))
    sums = jnp.concatenate([jnp.sum(product * product, axis=0), own_sums, jnp.zeros((1024 - 2 * cols,), F32)])
    sums = sums.reshape(8, 128)
    for axis in ("y", "x"):
        sums = jnp.sum(lax.all_to_all(jnp.broadcast_to(sums, (n, 8, 128)), axis, 0, 0), axis=0)
    sums = sums.reshape(1024)
    own_in = sums[cols : 2 * cols]
    expanded = product / own_in
    out_sums = sums[:cols] / (own_in * own_in)
    return (F32(order) * (expanded * expanded) / out_sums).astype(BF16)


def solution(mesh):
    fine = Mesh(mesh.devices.reshape(8, 8, 8, 2), ("x", "y", "z", "core"))
    cells = P(("x", "y"), ("z", "core"))

    return jax.shard_map(body, mesh=fine, in_specs=(cells, P(), P()), out_specs=cells, check_vma=False)
```

```python
import jax
import jax.numpy as jnp
from jax import lax
from jax.sharding import Mesh
from jax.sharding import PartitionSpec as P


BLK = 128
F32 = jnp.float32
BF16 = jnp.bfloat16
SCALE = 64.0


def local_mask(pattern, row_start, rows, col_start, cols):
    blocks = pattern.shape[0]
    row_blocks = (row_start + lax.broadcasted_iota(jnp.int32, (rows, blocks), 0)) // BLK
    pick_row = (row_blocks == lax.broadcasted_iota(jnp.int32, (rows, blocks), 1)).astype(BF16)
    col_blocks = (col_start + lax.broadcasted_iota(jnp.int32, (blocks, cols), 1)) // BLK
    pick_col = (col_blocks == lax.broadcasted_iota(jnp.int32, (blocks, cols), 0)).astype(BF16)
    eye = jnp.eye(blocks, dtype=jnp.int32)
    kept = jnp.maximum(pattern, eye).astype(BF16)
    by_row = jnp.dot(pick_row, kept, preferred_element_type=F32).astype(BF16)
    return jnp.dot(by_row, pick_col, preferred_element_type=F32) > 0.5


def split3(v):
    hi = v.astype(BF16)
    rest = v - hi.astype(F32)
    mid = rest.astype(BF16)
    return hi, mid, (rest - mid.astype(F32)).astype(BF16)


def body(similarity, in_pattern, out_pattern):
    rows, cols = similarity.shape
    x, y = lax.axis_index("x"), lax.axis_index("y")
    z, core = lax.axis_index("z"), lax.axis_index("core")
    n = lax.axis_size("x")
    order = rows * n * n
    row_start = (x * n + y) * rows
    col_start = (z * 2 + core) * cols
    in_mask = local_mask(in_pattern, row_start, rows, col_start, cols)
    masked = jnp.where(in_mask, similarity, jnp.zeros_like(similarity))
    half = rows // 2
    front = y < n // 2
    low, high = masked[:half], masked[half:]
    first = lax.ppermute(
        jnp.where(front, low, high), "y", [(i, 2 * i) if i < n // 2 else (i, 2 * i - n + 1) for i in range(n)]
    )
    second = lax.ppermute(
        jnp.where(front, high, low), "y", [(i, 2 * i + 1) if i < n // 2 else (i, 2 * i - n) for i in range(n)]
    )
    own_sums = jnp.sum(masked.astype(F32), axis=0)
    part = jnp.concatenate([own_sums, jnp.zeros((512 - cols,), F32)]).reshape(1, 4, 128)
    part = lax.all_to_all(jnp.broadcast_to(part, (n, 4, 128)), "x", 0, 0)
    part = jnp.sum(part, axis=0).reshape(1, 512)[:, :cols]
    left = jnp.concatenate([masked, *split3(part), jnp.zeros((128 - rows - 3, cols), BF16)])
    left = jnp.broadcast_to(left.T.reshape(n, 1, half, 128), (n, n, half, 128))
    left = lax.all_to_all(left.reshape(n * n, half, 128), ("y", "z"), 0, 0)
    left = left.reshape(n, cols, 128)
    right_all = lax.all_gather(jnp.concatenate([first, second]), "x")
    left, right_all = lax.optimization_barrier((left, right_all))
    in_sums = jnp.sum(jnp.sum(left[:, :, rows : rows + 3].astype(F32), axis=0), axis=1, keepdims=True)
    left_own = (left[:, :, :rows].astype(F32) / in_sums[None]).astype(BF16)
    left_other = lax.ppermute(left_own, "core", [(0, 1), (1, 0)])
    slot = (core + y) % 2
    halves = right_all.reshape(n, 2, half, cols)
    right_own = lax.dynamic_index_in_dim(halves, slot, 1, False).reshape(cols, cols)
    right_other = lax.dynamic_index_in_dim(halves, 1 - slot, 1, False).reshape(cols, cols)
    over_k = (((1,), (0,)), ((), ()))
    partial = lax.dot_general(left_own, right_own, over_k, preferred_element_type=F32)
    partial = partial + lax.dot_general(left_other, right_other, over_k, preferred_element_type=F32)
    partial = (partial * F32(SCALE)).astype(jnp.float16).reshape(n, rows, cols)
    partials = lax.all_to_all(partial, "y", 0, 0)
    product = jnp.sum(partials.astype(F32), axis=0) * F32(1.0 / SCALE)
    out_mask = local_mask(out_pattern, row_start, rows, col_start, cols)
    product = jnp.where(out_mask, product, F32(0.0))
    sums = jnp.concatenate([jnp.sum(product * product, axis=0), own_sums, jnp.zeros((1024 - 2 * cols,), F32)])
    sums = sums.reshape(8, 128)
    for axis in ("y", "x"):
        sums = jnp.sum(lax.all_to_all(jnp.broadcast_to(sums, (n, 8, 128)), axis, 0, 0), axis=0)
    sums = sums.reshape(1024)
    own_in = sums[cols : 2 * cols]
    expanded = product / own_in
    out_sums = sums[:cols] / (own_in * own_in)
    return (F32(order) * (expanded * expanded) / out_sums).astype(BF16)


def solution(mesh):
    fine = Mesh(mesh.devices.reshape(8, 8, 8, 2), ("x", "y", "z", "core"))
    cells = P(("x", "y"), ("z", "core"))

    return jax.shard_map(body, mesh=fine, in_specs=(cells, P(), P()), out_specs=cells, check_vma=False)
```

```python
import jax
import jax.numpy as jnp
from jax import lax
from jax.sharding import Mesh
from jax.sharding import PartitionSpec as P


BLK = 128
F32 = jnp.float32
BF16 = jnp.bfloat16
SCALE = 64.0


def local_mask(pattern, row_start, rows, col_start, cols):
    blocks = pattern.shape[0]
    row_blocks = (row_start + lax.broadcasted_iota(jnp.int32, (rows, blocks), 0)) // BLK
    pick_row = (row_blocks == lax.broadcasted_iota(jnp.int32, (rows, blocks), 1)).astype(BF16)
    col_blocks = (col_start + lax.broadcasted_iota(jnp.int32, (blocks, cols), 1)) // BLK
    pick_col = (col_blocks == lax.broadcasted_iota(jnp.int32, (blocks, cols), 0)).astype(BF16)
    eye = jnp.eye(blocks, dtype=jnp.int32)
    kept = jnp.maximum(pattern, eye).astype(BF16)
    by_row = jnp.dot(pick_row, kept, preferred_element_type=F32).astype(BF16)
    return jnp.dot(by_row, pick_col, preferred_element_type=F32) > 0.5


def body(similarity, in_pattern, out_pattern):
    rows, cols = similarity.shape
    x, y = lax.axis_index("x"), lax.axis_index("y")
    z, core = lax.axis_index("z"), lax.axis_index("core")
    n = lax.axis_size("x")
    order = rows * n * n
    row_start = (x * n + y) * rows
    col_start = (z * 2 + core) * cols
    in_mask = local_mask(in_pattern, row_start, rows, col_start, cols)
    masked = jnp.where(in_mask, similarity, jnp.zeros_like(similarity))
    own_sums = jnp.sum(masked.astype(F32), axis=0)
    half = rows // 2
    blocks = masked.T.reshape(n // 2, 2, half, rows)
    keep = jnp.where(core == 0, blocks[:, 0], blocks[:, 1])
    give = jnp.where(core == 0, blocks[:, 1], blocks[:, 0])
    got = lax.ppermute(give, "core", [(0, 1), (1, 0)])
    left = jnp.where(core == 0, jnp.concatenate([keep, got]), jnp.concatenate([got, keep]))
    left = jnp.broadcast_to(left[:, None], (n, n, half, rows))
    left = lax.all_to_all(left.reshape(n * n, half, rows), ("y", "z"), 0, 0)
    left = left.reshape(n, cols, rows)
    right_all = lax.all_gather(masked, "x", tiled=True)
    left, right_all = lax.optimization_barrier((left, right_all))
    part = jnp.sum(left.astype(F32), axis=(0, 2))
    part = jnp.concatenate([part, jnp.zeros((512 - cols,), F32)]).reshape(1, 4, 128)
    in_sums = lax.all_to_all(jnp.broadcast_to(part, (n, 4, 128)), "x", 0, 0)
    in_sums = jnp.sum(in_sums, axis=0).reshape(512)[:cols]
    left_own = (left.astype(F32) / in_sums[None, :, None]).astype(BF16)
    left_other = lax.ppermute(left_own, "core", [(0, 1), (1, 0)])
    halves = right_all.reshape(n, 2, half, cols)
    right_own = lax.dynamic_index_in_dim(halves, core, 1, False).reshape(cols, cols)
    right_other = lax.dynamic_index_in_dim(halves, 1 - core, 1, False).reshape(cols, cols)
    over_k = (((1,), (0,)), ((), ()))
    partial = lax.dot_general(left_own, right_own, over_k, preferred_element_type=F32)
    partial = partial + lax.dot_general(left_other, right_other, over_k, preferred_element_type=F32)
    partial = (partial * F32(SCALE)).astype(jnp.float16).reshape(n, rows, cols)
    partials = lax.all_to_all(partial, "y", 0, 0)
    product = jnp.sum(partials.astype(F32), axis=0) * F32(1.0 / SCALE)
    out_mask = local_mask(out_pattern, row_start, rows, col_start, cols)
    product = jnp.where(out_mask, product, F32(0.0))
    sums = jnp.concatenate([jnp.sum(product * product, axis=0), own_sums, jnp.zeros((1024 - 2 * cols,), F32)])
    sums = sums.reshape(8, 128)
    for axis in ("y", "x"):
        sums = jnp.sum(lax.all_to_all(jnp.broadcast_to(sums, (n, 8, 128)), axis, 0, 0), axis=0)
    sums = sums.reshape(1024)
    own_in = sums[cols : 2 * cols]
    expanded = product / own_in
    out_sums = sums[:cols] / (own_in * own_in)
    return (F32(order) * (expanded * expanded) / out_sums).astype(BF16)


def solution(mesh):
    fine = Mesh(mesh.devices.reshape(8, 8, 8, 2), ("x", "y", "z", "core"))
    cells = P(("x", "y"), ("z", "core"))

    return jax.shard_map(
        body, mesh=fine, in_specs=(cells, P(), P()), out_specs=cells, check_vma=False
    )
```

```python
import jax
import jax.numpy as jnp
from jax import lax
from jax.sharding import Mesh
from jax.sharding import PartitionSpec as P


BLK = 128
F32 = jnp.float32
BF16 = jnp.bfloat16
SCALE = 32.0

def local_mask(pattern, row_start, rows, col_start, cols):
    blocks = pattern.shape[0]
    row_blocks = (row_start + lax.broadcasted_iota(jnp.int32, (rows, blocks), 0)) // BLK
    pick_row = (row_blocks == lax.broadcasted_iota(jnp.int32, (rows, blocks), 1)).astype(BF16)
    col_blocks = (col_start + lax.broadcasted_iota(jnp.int32, (blocks, cols), 1)) // BLK
    pick_col = (col_blocks == lax.broadcasted_iota(jnp.int32, (blocks, cols), 0)).astype(BF16)
    eye = jnp.eye(blocks, dtype=jnp.int32)
    kept = jnp.maximum(pattern, eye).astype(BF16)
    by_row = jnp.dot(pick_row, kept, preferred_element_type=F32).astype(BF16)
    return jnp.dot(by_row, pick_col, preferred_element_type=F32) > 0.5

def send_all(v, axes, count):
    return jnp.sum(lax.all_to_all(jnp.broadcast_to(v, (count,) + v.shape), axes, 0, 0), axis=0)

def body(similarity, in_pattern, out_pattern):
    rows, cols = similarity.shape
    x, quad, spot = lax.axis_index("x"), lax.axis_index("quad"), lax.axis_index("spot")
    z, core = lax.axis_index("z"), lax.axis_index("core")
    n, m = lax.axis_size("x"), lax.axis_size("spot")
    order = rows * n * n
    row_start = (x * n + quad * m + spot) * rows
    col_start = (z * 2 + core) * cols
    swap = [(0, 1), (1, 0)]
    in_mask = local_mask(in_pattern, row_start, rows, col_start, cols)
    masked = jnp.where(in_mask, similarity, jnp.zeros_like(similarity))
    own_sums = jnp.sum(masked.astype(F32), axis=0)

    mine = masked.astype(jnp.float16)
    other = lax.ppermute(mine, "quad", swap)
    left = jnp.broadcast_to(masked.T.reshape(m, 1, rows, rows), (m, n, rows, rows))
    left = lax.all_to_all(left.reshape(m * n, rows, rows), ("spot", "z"), 0, 0)
    left = left.reshape(m, n, rows, rows)
    right = jnp.where(quad == 0, jnp.concatenate([mine, other]), jnp.concatenate([other, mine]))
    right = lax.all_gather(right, "x", tiled=True)
    left, right = lax.optimization_barrier((left, right))
    part = jnp.sum(left.astype(F32), axis=(0, 3))
    part = jnp.pad(part, ((0, 0), (0, 128 - rows)))
    in_sums = send_all(part, ("x", "quad"), 2 * n)[:, :rows, None]
    left_own = (left.astype(F32) / in_sums).astype(BF16)
    left_other = lax.ppermute(left_own, "core", swap)
    halves = right.reshape(n, 2, rows, cols)

    def times(l, which):
        r = lax.dynamic_index_in_dim(halves, which, 1, False).reshape(n * rows, cols).astype(BF16)
        l = l.reshape(m, n * rows, rows)
        return lax.dot_general(l, r, (((1,), (0,)), ((), ())), preferred_element_type=F32)

    partial = times(left_own, core) + times(left_other, 1 - core)
    partial = (partial * F32(SCALE)).astype(jnp.float16)
    partials = lax.all_to_all(partial, "spot", 0, 0)
    product = jnp.sum(partials.astype(F32), axis=0) * F32(1.0 / SCALE)
    out_mask = local_mask(out_pattern, row_start, rows, col_start, cols)
    product = jnp.where(out_mask, product, F32(0.0))
    sums = jnp.concatenate([jnp.sum(product * product, axis=0), own_sums, jnp.zeros((1024 - 2 * cols,), F32)])
    sums = send_all(send_all(sums.reshape(8, 128), ("quad", "spot"), n), "x", n).reshape(1024)
    own_in = sums[cols : 2 * cols]
    expanded = product / own_in
    out_sums = sums[:cols] / (own_in * own_in)
    return (F32(order) * (expanded * expanded) / out_sums).astype(BF16)

def solution(mesh):
    fine = Mesh(mesh.devices.reshape(8, 2, 4, 8, 2), ("x", "quad", "spot", "z", "core"))
    cells = P(("x", "quad", "spot"), ("z", "core"))

    return jax.shard_map(
        body, mesh=fine, in_specs=(cells, P(), P()), out_specs=cells, check_vma=False
    )
```

```python
import jax
import jax.numpy as jnp
from jax import lax
from jax.sharding import Mesh
from jax.sharding import PartitionSpec as P


BLK = 128
F32 = jnp.float32
BF16 = jnp.bfloat16
SCALE = 32.0

def local_mask(pattern, row_start, rows, col_start, cols):
    blocks = pattern.shape[0]
    row_blocks = (row_start + lax.broadcasted_iota(jnp.int32, (rows, blocks), 0)) // BLK
    pick_row = (row_blocks == lax.broadcasted_iota(jnp.int32, (rows, blocks), 1)).astype(BF16)
    col_blocks = (col_start + lax.broadcasted_iota(jnp.int32, (blocks, cols), 1)) // BLK
    pick_col = (col_blocks == lax.broadcasted_iota(jnp.int32, (blocks, cols), 0)).astype(BF16)
    eye = jnp.eye(blocks, dtype=jnp.int32)
    kept = jnp.maximum(pattern, eye).astype(BF16)
    by_row = jnp.dot(pick_row, kept, preferred_element_type=F32).astype(BF16)
    return jnp.dot(by_row, pick_col, preferred_element_type=F32) > 0.5

def send_all(v, axes, count):
    return jnp.sum(lax.all_to_all(jnp.broadcast_to(v, (count,) + v.shape), axes, 0, 0), axis=0)

def split3(v):
    hi = v.astype(BF16)
    rest = v - hi.astype(F32)
    mid = rest.astype(BF16)
    return hi, mid, (rest - mid.astype(F32)).astype(BF16)


def body(similarity, in_pattern, out_pattern):
    rows, cols = similarity.shape
    x, quad, spot = lax.axis_index("x"), lax.axis_index("quad"), lax.axis_index("spot")
    z, core = lax.axis_index("z"), lax.axis_index("core")
    n, m = lax.axis_size("x"), lax.axis_size("spot")
    order = rows * n * n
    row_start = (x * n + quad * m + spot) * rows
    col_start = (z * 2 + core) * cols
    swap = [(0, 1), (1, 0)]
    in_mask = local_mask(in_pattern, row_start, rows, col_start, cols)
    masked = jnp.where(in_mask, similarity, jnp.zeros_like(similarity))
    own_sums = jnp.sum(masked.astype(F32), axis=0)

    mine = masked.astype(jnp.float16)
    other = lax.ppermute(mine, "quad", swap)
    part = jnp.pad(own_sums, (0, 512 - cols)).reshape(4, 128)
    part = send_all(part, ("x", "quad"), 2 * n).reshape(1, 512)[:, :cols]
    left = jnp.concatenate([masked, *split3(part), jnp.zeros((128 - rows - 3, cols), BF16)])
    left = jnp.broadcast_to(left.T.reshape(m, 1, rows, 128), (m, n, rows, 128))
    left = lax.all_to_all(left.reshape(m * n, rows, 128), ("spot", "z"), 0, 0)
    left = left.reshape(m, n, rows, 128)
    right = jnp.where(quad == 0, jnp.concatenate([mine, other]), jnp.concatenate([other, mine]))
    right = lax.all_gather(right, "x", tiled=True)
    left, right = lax.optimization_barrier((left, right))
    in_sums = jnp.sum(jnp.sum(left[..., rows : rows + 3].astype(F32), axis=0), axis=-1, keepdims=True)
    left_own = (left[..., :rows].astype(F32) / in_sums).astype(BF16)
    left_other = lax.ppermute(left_own, "core", swap)
    halves = right.reshape(n, 2, rows, cols)

    def times(l, which):
        r = lax.dynamic_index_in_dim(halves, which, 1, False).reshape(n * rows, cols).astype(BF16)
        l = l.reshape(m, n * rows, rows)
        return lax.dot_general(l, r, (((1,), (0,)), ((), ())), preferred_element_type=F32)

    partial = times(left_own, core) + times(left_other, 1 - core)
    partial = (partial * F32(SCALE)).astype(jnp.float16)
    partials = lax.all_to_all(partial, "spot", 0, 0)
    product = jnp.sum(partials.astype(F32), axis=0) * F32(1.0 / SCALE)
    out_mask = local_mask(out_pattern, row_start, rows, col_start, cols)
    product = jnp.where(out_mask, product, F32(0.0))
    sums = jnp.concatenate([jnp.sum(product * product, axis=0), own_sums, jnp.zeros((1024 - 2 * cols,), F32)])
    sums = send_all(sums.reshape(8, 128), ("x", "quad", "spot"), n * n).reshape(1024)
    own_in = sums[cols : 2 * cols]
    expanded = product / own_in
    out_sums = sums[:cols] / (own_in * own_in)
    return (F32(order) * (expanded * expanded) / out_sums).astype(BF16)

def solution(mesh):
    fine = Mesh(mesh.devices.reshape(8, 2, 4, 8, 2), ("x", "quad", "spot", "z", "core"))
    cells = P(("x", "quad", "spot"), ("z", "core"))

    return jax.shard_map(body, mesh=fine, in_specs=(cells, P(), P()), out_specs=cells, check_vma=False)
```

```python
import jax
import jax.numpy as jnp
from jax import lax
from jax.sharding import Mesh
from jax.sharding import PartitionSpec as P


BLK = 128
F32 = jnp.float32
BF16 = jnp.bfloat16
SCALE = 32.0

def local_mask(pattern, row_start, rows, col_start, cols):
    blocks = pattern.shape[0]
    row_blocks = (row_start + lax.broadcasted_iota(jnp.int32, (rows, blocks), 0)) // BLK
    pick_row = (row_blocks == lax.broadcasted_iota(jnp.int32, (rows, blocks), 1)).astype(BF16)
    col_blocks = (col_start + lax.broadcasted_iota(jnp.int32, (blocks, cols), 1)) // BLK
    pick_col = (col_blocks == lax.broadcasted_iota(jnp.int32, (blocks, cols), 0)).astype(BF16)
    eye = jnp.eye(blocks, dtype=jnp.int32)
    kept = jnp.maximum(pattern, eye).astype(BF16)
    by_row = jnp.dot(pick_row, kept, preferred_element_type=F32).astype(BF16)
    return jnp.dot(by_row, pick_col, preferred_element_type=F32) > 0.5

def send_all(v, axes, count):
    return jnp.sum(lax.all_to_all(jnp.broadcast_to(v, (count,) + v.shape), axes, 0, 0), axis=0)

def split3(v):
    hi = v.astype(BF16)
    rest = v - hi.astype(F32)
    mid = rest.astype(BF16)
    return hi, mid, (rest - mid.astype(F32)).astype(BF16)


def body(similarity, in_pattern, out_pattern):
    rows, cols = similarity.shape
    x, quad, spot = lax.axis_index("x"), lax.axis_index("quad"), lax.axis_index("spot")
    z, core = lax.axis_index("z"), lax.axis_index("core")
    n, m = lax.axis_size("x"), lax.axis_size("spot")
    order = rows * n * n
    row_start = (x * n + quad * m + spot) * rows
    col_start = (z * 2 + core) * cols
    swap = [(0, 1), (1, 0)]
    in_mask = local_mask(in_pattern, row_start, rows, col_start, cols)
    masked = jnp.where(in_mask, similarity, jnp.zeros_like(similarity))
    own_sums = jnp.sum(masked.astype(F32), axis=0)

    mine = masked.astype(jnp.float16)
    other = lax.ppermute(mine, "quad", swap)
    part = jnp.pad(own_sums, (0, 512 - cols)).reshape(4, 128)
    part = send_all(part, ("x", "quad"), 2 * n).reshape(1, 512)[:, :cols]
    left = jnp.concatenate([masked, *split3(part), jnp.zeros((128 - rows - 3, cols), BF16)])
    left = jnp.broadcast_to(left.T.reshape(m, 1, rows, 128), (m, n, rows, 128))
    left = lax.all_to_all(left.reshape(m * n, rows, 128), ("spot", "z"), 0, 0)
    left = left.reshape(m, n, rows, 128)
    right = jnp.where(quad == 0, jnp.concatenate([mine, other]), jnp.concatenate([other, mine]))
    right = lax.all_gather(right, "x", tiled=True)
    left, right = lax.optimization_barrier((left, right))
    other = lax.ppermute(left, "core", swap)
    halves = right.reshape(n, 2, rows, cols)

    def times(l, which):
        in_sums = jnp.sum(jnp.sum(l[..., rows : rows + 3].astype(F32), axis=0), axis=-1, keepdims=True)
        r = lax.dynamic_index_in_dim(halves, which, 1, False).astype(F32) / in_sums
        r = r.astype(BF16).reshape(n * rows, cols)
        l = l.reshape(m, n * rows, 128)
        return lax.dot_general(l, r, (((1,), (0,)), ((), ())), preferred_element_type=F32)

    partial = (times(left, core) + times(other, 1 - core))[:, :rows]
    partial = (partial * F32(SCALE)).astype(jnp.float16)
    partials = lax.all_to_all(partial, "spot", 0, 0)
    product = jnp.sum(partials.astype(F32), axis=0) * F32(1.0 / SCALE)
    out_mask = local_mask(out_pattern, row_start, rows, col_start, cols)
    product = jnp.where(out_mask, product, F32(0.0))
    sums = jnp.concatenate([jnp.sum(product * product, axis=0), own_sums, jnp.zeros((1024 - 2 * cols,), F32)])
    sums = send_all(sums.reshape(8, 128), ("x", "quad", "spot"), n * n).reshape(1024)
    own_in = sums[cols : 2 * cols]
    expanded = product / own_in
    out_sums = sums[:cols] / (own_in * own_in)
    return (F32(order) * (expanded * expanded) / out_sums).astype(BF16)

def solution(mesh):
    fine = Mesh(mesh.devices.reshape(8, 2, 4, 8, 2), ("x", "quad", "spot", "z", "core"))
    cells = P(("x", "quad", "spot"), ("z", "core"))

    return jax.shard_map(body, mesh=fine, in_specs=(cells, P(), P()), out_specs=cells, check_vma=False)
```
